32 devices in a mesh: col: 8 (over y, x, core), dev: 4 (over z).
Axes of the slice: x: 2, y: 2, z: 4, core: 2. Of those that a mesh axis runs over, the one named last changes fastest.
Arguments:
- first_factor: bfloat16 [16, 1024, 2048], P(None, 'col', 'dev'), may hold values from -1 to 1
- second_factor: bfloat16 [16, 1024, 2048], P(None, 'dev', 'col'), may hold values from -1 to 1
- amplitudes: bfloat16 [512, 1024, 1024], P(None, 'col', 'dev'), may hold values from -0.0059814453 to 0.0059814453
Outputs:
- ladder: float32 [512, 256], P(('col', 'dev'))
The draws below stay inside these ranges and needn't reach their ends.
All inputs are finite; a program needn't handle non-finite values.
Results may differ from the reference program's by a relative error of at most 0.0029.
Values may be sent and summed in bfloat16 or wider, within the bound.
A program may use at most 128 MiB of HBM per device.

```python
import jax
import jax.numpy as jnp
from jax import lax

V = 1024
Q = 2048
P_SIZE = 512
WA = 16
WB = 16


def with_spikes(entries, key, source, target, shards_of, factor):
    owner, partner = [(jnp.arange(entries.shape[position]) // (entries.shape[position] // shards_of)).reshape([-1 if axis == position else 1 for axis in range(entries.ndim)]) for position in (source, target)]
    chosen = jax.random.permutation(key, shards_of)[partner]
    strong = (owner == chosen) | (owner == (partner + shards_of // 2) % shards_of)
    return jnp.where(strong, factor * entries, entries)


def block_scale(stream_key, dims, pieces, low, top_value):
    def one(position, shards_of):
        heights = jax.random.uniform(jax.random.fold_in(jax.random.fold_in(stream_key, 6), position), (shards_of,), jnp.float32, low / len(pieces), top_value / len(pieces))
        return jnp.repeat(jnp.exp(heights), dims[position] // shards_of).reshape((-1,) + (1,) * (len(dims) - position - 1))

    gain = one(*pieces[0])
    for cut in pieces[1:]:
        gain = gain * one(*cut)
    return gain


def gaussian(own_key, extent, scale, most, cuts=(), kind=jnp.bfloat16):
    array = jax.random.normal(own_key, extent, jnp.float32) * scale
    if len(cuts) > 0:
        array = block_scale(own_key, extent, cuts, -0.22, 0.18) * array
    return jnp.clip(array, min=-most, max=most).astype(kind)


def bell_draw_with(own_key, shape, spread, reach, cuts, heavy, kind=jnp.bfloat16):
    array = spread * jax.random.normal(own_key, shape, jnp.float32)
    if cuts:
        array = array * block_scale(own_key, shape, cuts, -0.22, 0.18)
    return jnp.clip(with_spikes(array, jax.random.fold_in(own_key, 3), *heavy), -reach, reach).astype(kind)


def setup_inputs(seed: int = 0) -> dict:
    arg_keys = jax.random.split(jax.random.key(seed), 4)
    first_factor = gaussian(arg_keys[0], (WA, V, Q), 0.1487, 1.0, ((1, 8), (2, 4)))
    second_factor = gaussian(arg_keys[1], (WB, V, Q), 0.1487, 1.0, ((1, 4), (2, 8)))
    amplitudes = bell_draw_with(arg_keys[2], (P_SIZE, V, V), 0.0009765625, 0.0059814453, ((1, 8), (2, 4)), (1, 0, 8, 2.0))
    return dict(first_factor=first_factor, second_factor=second_factor, amplitudes=amplitudes)


def reference(first_factor, second_factor, amplitudes):
    second_flat = second_factor.reshape(WB * V, Q)
    amp_flat = amplitudes.reshape(P_SIZE, V * V)

    def one_row(first_row):
        tile = jnp.dot(first_row, second_flat.T, preferred_element_type=jnp.float32).astype(jnp.bfloat16)
        tile = tile.reshape(V, WB, V).transpose(1, 0, 2).reshape(WB, V * V)
        return jnp.dot(amp_flat, tile.T, preferred_element_type=jnp.float32)

    rows = lax.map(one_row, first_factor)
    return rows.transpose(1, 0, 2).reshape(P_SIZE, WA * WB)
```

```python
import functools

import jax
import jax.numpy as jnp
from jax import lax
from jax.experimental import pallas as pl
from jax.experimental.pallas import tpu as pltpu
from jax.sharding import PartitionSpec as P

MESH = pl.DeviceIdType.MESH
CHUNKS = 8
AHEAD = 2
NT = (((1,), (1,)), ((), ()))


def kernel(
    ncol, ndev, first, second, amps, out,
    first_all, second_all, raw, turned, tile, total, parts, final, half_sum,
    own_sem, z_send, z_recv, r_send, r_recv, c_send, c_recv, t_sem, s_send, s_recv, d_send, d_recv,
):
    col, dev = lax.axis_index("col"), lax.axis_index("dev")
    n_c, n_a, q_first = first.shape
    n_b, n_d, q_second = second.shape
    pairs = amps.shape[0]
    size = n_c // CHUNKS
    chips = ncol // 2
    far = chips // 2
    core, chip = lax.rem(col, 2), col // 2

    def swap(spot):
        return jnp.where(spot < far, spot, 3 * far - 1 - spot)

    spot = swap(chip)

    def at_spot(offset):
        return swap(lax.rem(spot + offset + 2 * chips, chips)) * 2 + core

    partner = chip * 2 + 1 - core

    barrier = pltpu.get_barrier_semaphore()
    for off in range(1, ncol):
        pl.semaphore_signal(
            barrier, inc=1, device_id={"col": lax.rem(col + off, ncol)}, device_id_type=MESH
        )
    for off in range(1, ndev):
        pl.semaphore_signal(
            barrier, inc=1, device_id={"dev": lax.rem(dev + off, ndev)}, device_id_type=MESH
        )
    pl.semaphore_wait(barrier, ncol + ndev - 2)

    def z_slice(source, k):
        return first_all.at[
            pl.ds(k * size, size), :, pl.ds(pl.multiple_of(source * q_first, q_first), q_first)
        ]

    def z_copy(way, hop, k):
        step = 1 if way == 0 else -1
        source = dev - step * (hop - 1)
        src = first.at[pl.ds(k * size, size)] if hop == 1 else z_slice(source, k)
        return pltpu.make_async_remote_copy(
            src_ref=src,
            dst_ref=z_slice(source, k),
            send_sem=z_send.at[way, hop - 1, k],
            recv_sem=z_recv.at[way, hop - 1, k],
            device_id={"dev": dev + step},
            device_id_type=MESH,
        )

    def z_arrival(way, hop, k):
        step = 1 if way == 0 else -1
        here = z_slice(dev - step * hop, k)
        return pltpu.make_async_copy(here, here, z_recv.at[way, hop - 1, k])

    def sends(way, hop):
        if way == 0:
            return (dev - (hop - 1) >= 0) & (dev + 1 < ndev)
        return (dev + (hop - 1) < ndev) & (dev - 1 >= 0)

    def receives(way, hop):
        return (dev - hop >= 0) if way == 0 else (dev + hop < ndev)

    def z_own(k):
        for way in range(2):
            @pl.when(sends(way, 1))
            def _():
                z_copy(way, 1, k).start()

    def z_round(k):
        @pl.when(k + AHEAD < CHUNKS)
        def _():
            z_own(k + AHEAD)

        for hop in range(1, ndev):
            for way in range(2):
                @pl.when(receives(way, hop))
                def _():
                    z_arrival(way, hop, k).wait()

                if hop + 1 < ndev:
                    @pl.when(sends(way, hop + 1))
                    def _():
                        z_copy(way, hop + 1, k).start()

    wide = n_b // 2

    def p_slice(source, h):
        return second_all.at[
            pl.ds(h * wide, wide), :, pl.ds(pl.multiple_of(source * q_second, q_second), q_second)
        ]

    def p_source(way, hop):
        return at_spot(-hop if way == 0 else hop)

    def r_copy(way, hop, h):
        source = p_source(way, hop - 1)
        src = second.at[pl.ds(h * wide, wide)] if hop == 1 else p_slice(source, h)
        return pltpu.make_async_remote_copy(
            src_ref=src,
            dst_ref=p_slice(source, h),
            send_sem=r_send.at[way, hop - 1, h],
            recv_sem=r_recv.at[way, hop - 1, h],
            device_id={"col": at_spot(1 if way == 0 else -1)},
            device_id_type=MESH,
        )

    def r_arrival(way, hop, h):
        here = p_slice(p_source(way, hop), h)
        return pltpu.make_async_copy(here, here, r_recv.at[way, hop - 1, h])

    def c_copy(way, hop, h):
        source = p_source(way, hop)
        src = second.at[pl.ds(h * wide, wide)] if hop == 0 else p_slice(source, h)
        return pltpu.make_async_remote_copy(
            src_ref=src,
            dst_ref=p_slice(source, h),
            send_sem=c_send.at[way, hop, h],
            recv_sem=c_recv.at[way, hop, h],
            device_id={"col": partner},
            device_id_type=MESH,
        )

    def c_arrival(way, hop, h):
        source = p_source(way, hop) + 1 - 2 * core
        here = p_slice(source, h)
        return pltpu.make_async_copy(here, here, c_recv.at[way, hop, h])

    def travels(way, hop):
        if hop < far:
            return (0, 1) if way == 0 else (1, 0)
        return (way,) if hop == far else ()

    pieces = [
        (way, hop, travels(way, hop)[place])
        for hop in range(1, far + 1)
        for place in range(len(travels(0, hop)))
        for way in range(2)
    ]
    shared = [(0, 0, 0), (0, 0, 1)] + pieces

    own_first = pltpu.make_async_copy(
        first, first_all.at[:, :, pl.ds(pl.multiple_of(dev * q_first, q_first), q_first)],
        own_sem.at[0],
    )
    own_second = pltpu.make_async_copy(
        second, second_all.at[:, :, pl.ds(pl.multiple_of(col * q_second, q_second), q_second)],
        own_sem.at[1],
    )

    def t_copy(k):
        slot = lax.rem(k, 2)
        return pltpu.make_async_copy(
            amps.at[:, pl.ds(pl.multiple_of(k * size, size), size), :], raw.at[slot],
            t_sem.at[slot],
        )

    for k in range(AHEAD):
        z_own(k)
    for way, hop, h in pieces:
        if hop == 1:
            r_copy(way, 1, h).start()
    own_first.start()
    own_second.start()
    t_copy(0).start()
    for h in range(2):
        c_copy(0, 0, h).start()

    lead = CHUNKS // 2
    by_round = [[] for _ in range(lead)]
    for number, piece in enumerate(pieces):
        by_round[min(lead - 1, 1 + number * lead // len(pieces))].append(piece)

    def take(way, hop, h):
        r_arrival(way, hop, h).wait()
        if h in travels(way, hop + 1):
            r_copy(way, hop + 1, h).start()
        c_copy(way, hop, h).start()

    for k in range(lead):
        for piece in by_round[k]:
            take(*piece)
        z_round(k)
    own_first.wait()
    own_second.wait()
    for piece in shared:
        c_arrival(*piece).wait()

    total[...] = jnp.zeros_like(total)

    def one_block(k, _):
        slot = lax.rem(k, 2)
        t_copy(k).wait()

        @pl.when(k + 1 < CHUNKS)
        def _():
            t_copy(k + 1).start()

        def turn(i, _):
            rows = pl.ds(pl.multiple_of(i * 16, 16), 16)
            turned[:, rows, :] = jnp.swapaxes(raw[slot, rows], 0, 1)
            return 0

        lax.fori_loop(0, pairs // 16, turn, 0)

        def one_b(b, _):
            left = first_all[pl.ds(k * size, size)].reshape(size * n_a, -1)
            got = lax.dot_general(left, second_all[b], NT, preferred_element_type=jnp.float32)
            tile[:, b] = got.astype(jnp.bfloat16).reshape(size, n_a, n_d)
            return 0

        lax.fori_loop(0, n_b, one_b, 0)

        def one_c(c, _):
            total[...] += lax.dot_general(
                turned[c], tile[c].reshape(n_b * n_a, n_d), NT, preferred_element_type=jnp.float32
            )
            return 0

        lax.fori_loop(0, size, one_c, 0)

        @pl.when(((lax.rem(k, 2) == 1) & (k < CHUNKS - 1)) | (k == CHUNKS - 2))
        def _():
            z_round(lead + k // 2)

        return 0

    lax.fori_loop(0, CHUNKS, one_block, 0)

    some = pairs // ncol

    def s_copy(off):
        to = lax.rem(col + off, ncol)
        return pltpu.make_async_remote_copy(
            src_ref=total.at[pl.ds(pl.multiple_of(to * some, some), some)],
            dst_ref=parts.at[off],
            send_sem=s_send.at[off],
            recv_sem=s_recv.at[off],
            device_id={"col": to},
            device_id_type=MESH,
        )

    for off in range(1, ncol):
        s_copy(off).start()
    mine = total[pl.ds(pl.multiple_of(col * some, some), some), :]
    for off in range(1, ncol):
        s_copy(off).wait_recv()
        mine += parts[off]
    half_sum[...] = mine.reshape(half_sum.shape)

    def d_copy(off):
        to = lax.rem(dev + off, ndev)
        return pltpu.make_async_remote_copy(
            src_ref=half_sum.at[to],
            dst_ref=final.at[off],
            send_sem=d_send.at[off],
            recv_sem=d_recv.at[off],
            device_id={"dev": to},
            device_id_type=MESH,
        )

    for off in range(1, ndev):
        d_copy(off).start()
    result = half_sum[dev]
    for off in range(1, ndev):
        d_copy(off).wait_recv()
        result += final[off]
    out[...] = result

    for off in range(1, ncol):
        s_copy(off).wait_send()
    for off in range(1, ndev):
        d_copy(off).wait_send()
    for piece in pieces:
        r_copy(*piece).wait_send()
    for piece in shared:
        c_copy(*piece).wait_send()

    def drain(k, _):
        for way in range(2):
            for hop in range(1, ndev):
                @pl.when(sends(way, hop))
                def _():
                    z_copy(way, hop, k).wait_send()
        return 0

    lax.fori_loop(0, CHUNKS, drain, 0)


def on_device(ncol, ndev, first_factor, second_factor, amplitudes):
    n_a, n_c, q_first = first_factor.shape
    n_b, n_d, q_second = second_factor.shape
    pairs = amplitudes.shape[0]
    size = n_c // CHUNKS
    far = ncol // 4
    whole = q_first * ndev
    some = pairs // ncol
    few = some // ndev
    width = n_a * n_b
    anywhere = pl.BlockSpec(memory_space=pl.ANY)
    dma = pltpu.SemaphoreType.DMA
    got = pl.pallas_call(
        functools.partial(kernel, ncol, ndev),
        out_shape=jax.ShapeDtypeStruct((few, width), jnp.float32),
        in_specs=[anywhere] * 3,
        out_specs=pl.BlockSpec(memory_space=pltpu.VMEM),
        scratch_shapes=[
            pltpu.VMEM((n_c, n_a, whole), jnp.bfloat16),
            pltpu.VMEM((n_b, n_d, whole), jnp.bfloat16),
            pltpu.VMEM((2, pairs, size, n_d), jnp.bfloat16),
            pltpu.VMEM((size, pairs, n_d), jnp.bfloat16),
            pltpu.VMEM((size, n_b, n_a, n_d), jnp.bfloat16),
            pltpu.VMEM((pairs, width), jnp.float32),
            pltpu.VMEM((ncol, some, width), jnp.float32),
            pltpu.VMEM((ndev, few, width), jnp.float32),
            pltpu.VMEM((ndev, few, width), jnp.float32),
            dma((2,)),
            dma((2, ndev - 1, CHUNKS)),
            dma((2, ndev - 1, CHUNKS)),
            dma((2, far, 2)),
            dma((2, far, 2)),
            dma((2, far + 1, 2)),
            dma((2, far + 1, 2)),
            dma((2,)),
            dma((ncol,)),
            dma((ncol,)),
            dma((ndev,)),
            dma((ndev,)),
        ],
        compiler_params=pltpu.CompilerParams(
            collective_id=0, has_side_effects=True, vmem_limit_bytes=58 * 2**20
        ),
    )(jnp.swapaxes(first_factor, 0, 1), second_factor, amplitudes)
    return jnp.swapaxes(got.reshape(few, n_b, n_a), 1, 2).reshape(few, width)


def solution(mesh):
    placed = (P(None, "col", "dev"), P(None, "dev", "col"), P(None, "col", "dev"))
    return jax.shard_map(
        functools.partial(on_device, mesh.shape["col"], mesh.shape["dev"]),
        mesh=mesh, in_specs=placed, out_specs=P(("col", "dev"), None), check_vma=False,
    )
```

```python
import functools

import jax
import jax.numpy as jnp
from jax import lax
from jax.experimental import pallas as pl
from jax.experimental.pallas import tpu as pltpu
from jax.sharding import PartitionSpec as P

MESH = pl.DeviceIdType.MESH
CHUNKS = 8
AHEAD = 2
GROUP = 8
WIDE = 8
NT = (((1,), (1,)), ((), ()))


def kernel(
    ncol, ndev, first, second, amps, out,
    first_all, second_all, raw, turned, tile, total, parts, final, half_sum,
    own_sem, z_send, z_recv, r_send, r_recv, c_send, c_recv, t_sem, s_send, s_recv, d_send, d_recv,
):
    col, dev = lax.axis_index("col"), lax.axis_index("dev")
    n_c, n_a, q_first = first.shape
    n_b, n_d, q_second = second.shape
    pairs = amps.shape[0]
    size = n_c // CHUNKS
    chips = ncol // 2
    far = chips // 2
    core, chip = lax.rem(col, 2), col // 2

    def swap(spot):
        return jnp.where(spot < far, spot, 3 * far - 1 - spot)

    spot = swap(chip)

    def at_spot(offset):
        return swap(lax.rem(spot + offset + 2 * chips, chips)) * 2 + core

    partner = chip * 2 + 1 - core

    barrier = pltpu.get_barrier_semaphore()
    for off in range(1, ncol):
        pl.semaphore_signal(
            barrier, inc=1, device_id={"col": lax.rem(col + off, ncol)}, device_id_type=MESH
        )
    for off in range(1, ndev):
        pl.semaphore_signal(
            barrier, inc=1, device_id={"dev": lax.rem(dev + off, ndev)}, device_id_type=MESH
        )
    pl.semaphore_wait(barrier, ncol + ndev - 2)

    def z_slice(source, k):
        return first_all.at[
            pl.ds(k * size, size), :, pl.ds(pl.multiple_of(source * q_first, q_first), q_first)
        ]

    def z_copy(way, hop, k):
        step = 1 if way == 0 else -1
        source = dev - step * (hop - 1)
        src = first.at[pl.ds(k * size, size)] if hop == 1 else z_slice(source, k)
        return pltpu.make_async_remote_copy(
            src_ref=src,
            dst_ref=z_slice(source, k),
            send_sem=z_send.at[way, hop - 1, k],
            recv_sem=z_recv.at[way, hop - 1, k],
            device_id={"dev": dev + step},
            device_id_type=MESH,
        )

    def z_arrival(way, hop, k):
        step = 1 if way == 0 else -1
        here = z_slice(dev - step * hop, k)
        return pltpu.make_async_copy(here, here, z_recv.at[way, hop - 1, k])

    def sends(way, hop):
        if way == 0:
            return (dev - (hop - 1) >= 0) & (dev + 1 < ndev)
        return (dev + (hop - 1) < ndev) & (dev - 1 >= 0)

    def receives(way, hop):
        return (dev - hop >= 0) if way == 0 else (dev + hop < ndev)

    def z_own(k):
        for way in range(2):
            @pl.when(sends(way, 1))
            def _():
                z_copy(way, 1, k).start()

    def z_round(k):
        @pl.when(k + AHEAD < CHUNKS)
        def _():
            z_own(k + AHEAD)

        for hop in range(1, ndev):
            for way in range(2):
                @pl.when(receives(way, hop))
                def _():
                    z_arrival(way, hop, k).wait()

                if hop + 1 < ndev:
                    @pl.when(sends(way, hop + 1))
                    def _():
                        z_copy(way, hop + 1, k).start()

    wide = n_b // 2

    def p_slice(source, h):
        return second_all.at[
            pl.ds(h * wide, wide), :, pl.ds(pl.multiple_of(source * q_second, q_second), q_second)
        ]

    def p_source(way, hop):
        return at_spot(-hop if way == 0 else hop)

    def r_copy(way, hop, h):
        source = p_source(way, hop - 1)
        src = second.at[pl.ds(h * wide, wide)] if hop == 1 else p_slice(source, h)
        return pltpu.make_async_remote_copy(
            src_ref=src,
            dst_ref=p_slice(source, h),
            send_sem=r_send.at[way, hop - 1, h],
            recv_sem=r_recv.at[way, hop - 1, h],
            device_id={"col": at_spot(1 if way == 0 else -1)},
            device_id_type=MESH,
        )

    def r_arrival(way, hop, h):
        here = p_slice(p_source(way, hop), h)
        return pltpu.make_async_copy(here, here, r_recv.at[way, hop - 1, h])

    def c_copy(way, hop, h):
        source = p_source(way, hop)
        src = second.at[pl.ds(h * wide, wide)] if hop == 0 else p_slice(source, h)
        return pltpu.make_async_remote_copy(
            src_ref=src,
            dst_ref=p_slice(source, h),
            send_sem=c_send.at[way, hop, h],
            recv_sem=c_recv.at[way, hop, h],
            device_id={"col": partner},
            device_id_type=MESH,
        )

    def c_arrival(way, hop, h):
        source = p_source(way, hop) + 1 - 2 * core
        here = p_slice(source, h)
        return pltpu.make_async_copy(here, here, c_recv.at[way, hop, h])

    def travels(way, hop):
        if hop < far:
            return (0, 1) if way == 0 else (1, 0)
        return (way,) if hop == far else ()

    pieces = [
        (way, hop, travels(way, hop)[place])
        for hop in range(1, far + 1)
        for place in range(len(travels(0, hop)))
        for way in range(2)
    ]
    shared = [(0, 0, 0), (0, 0, 1)] + pieces

    own_first = pltpu.make_async_copy(
        first, first_all.at[:, :, pl.ds(pl.multiple_of(dev * q_first, q_first), q_first)],
        own_sem.at[0],
    )
    own_second = pltpu.make_async_copy(
        second, second_all.at[:, :, pl.ds(pl.multiple_of(col * q_second, q_second), q_second)],
        own_sem.at[1],
    )

    def t_copy(k):
        slot = lax.rem(k, 2)
        return pltpu.make_async_copy(
            amps.at[:, pl.ds(pl.multiple_of(k * size, size), size), :], raw.at[slot],
            t_sem.at[slot],
        )

    for k in range(AHEAD):
        z_own(k)
    for way, hop, h in pieces:
        if hop == 1:
            r_copy(way, 1, h).start()
    own_first.start()
    own_second.start()
    t_copy(0).start()
    for h in range(2):
        c_copy(0, 0, h).start()

    lead = CHUNKS // 2
    by_round = [[] for _ in range(lead)]
    for number, piece in enumerate(pieces):
        by_round[min(lead - 1, 1 + number * lead // len(pieces))].append(piece)

    def take(way, hop, h):
        r_arrival(way, hop, h).wait()
        if h in travels(way, hop + 1):
            r_copy(way, hop + 1, h).start()
        c_copy(way, hop, h).start()

    def turn_block(k):
        slot, held = lax.rem(k, 2), lax.rem(k, lead)
        t_copy(k).wait()

        @pl.when(k + 1 < CHUNKS)
        def _():
            t_copy(k + 1).start()

        def turn(i, _):
            rows = pl.ds(pl.multiple_of(i * 16, 16), 16)
            turned[held, :, rows, :] = jnp.swapaxes(raw[slot, rows], 0, 1)
            return 0

        lax.fori_loop(0, pairs // 16, turn, 0)

    for k in range(lead):
        turn_block(k)
        for piece in by_round[k]:
            take(*piece)
        z_round(k)
    own_first.wait()
    own_second.wait()
    for piece in shared:
        c_arrival(*piece).wait()

    total[...] = jnp.zeros_like(total)

    def one_block(k, _):
        held = lax.rem(k, lead)

        def one_b(b, _):
            left = first_all[pl.ds(k * size, size)].reshape(size * n_a, -1)
            right = second_all[pl.ds(b * WIDE, WIDE)].reshape(WIDE * n_d, -1)
            got = lax.dot_general(left, right, NT, preferred_element_type=jnp.float32)
            got = got.astype(jnp.bfloat16)
            for i in range(WIDE):
                tile[:, b * WIDE + i] = got[:, i * n_d : (i + 1) * n_d].reshape(size, n_a, n_d)
            return 0

        lax.fori_loop(0, n_b // WIDE, one_b, 0)

        def some_c(g, _):
            group = [g * GROUP + i for i in range(GROUP)]
            left = jnp.concatenate([turned[held, c] for c in group], axis=1)
            right = jnp.concatenate([tile[c].reshape(n_b * n_a, n_d) for c in group], axis=1)
            total[...] += lax.dot_general(left, right, NT, preferred_element_type=jnp.float32)
            return 0

        lax.fori_loop(0, size // GROUP, some_c, 0)

        @pl.when(k + lead < CHUNKS)
        def _():
            turn_block(k + lead)

        @pl.when(((lax.rem(k, 2) == 1) & (k < CHUNKS - 1)) | (k == CHUNKS - 2))
        def _():
            z_round(lead + k // 2)

        return 0

    lax.fori_loop(0, CHUNKS, one_block, 0)

    some = pairs // ncol

    def s_copy(off):
        to = lax.rem(col + off, ncol)
        return pltpu.make_async_remote_copy(
            src_ref=total.at[pl.ds(pl.multiple_of(to * some, some), some)],
            dst_ref=parts.at[off],
            send_sem=s_send.at[off],
            recv_sem=s_recv.at[off],
            device_id={"col": to},
            device_id_type=MESH,
        )

    for off in range(1, ncol):
        s_copy(off).start()
    mine = total[pl.ds(pl.multiple_of(col * some, some), some), :]
    for off in range(1, ncol):
        s_copy(off).wait_recv()
        mine += parts[off]
    half_sum[...] = mine.reshape(half_sum.shape)

    def d_copy(off):
        to = lax.rem(dev + off, ndev)
        return pltpu.make_async_remote_copy(
            src_ref=half_sum.at[to],
            dst_ref=final.at[off],
            send_sem=d_send.at[off],
            recv_sem=d_recv.at[off],
            device_id={"dev": to},
            device_id_type=MESH,
        )

    for off in range(1, ndev):
        d_copy(off).start()
    result = half_sum[dev]
    for off in range(1, ndev):
        d_copy(off).wait_recv()
        result += final[off]
    out[...] = result

    for off in range(1, ncol):
        s_copy(off).wait_send()
    for off in range(1, ndev):
        d_copy(off).wait_send()
    for piece in pieces:
        r_copy(*piece).wait_send()
    for piece in shared:
        c_copy(*piece).wait_send()

    def drain(k, _):
        for way in range(2):
            for hop in range(1, ndev):
                @pl.when(sends(way, hop))
                def _():
                    z_copy(way, hop, k).wait_send()
        return 0

    lax.fori_loop(0, CHUNKS, drain, 0)


def on_device(ncol, ndev, first_factor, second_factor, amplitudes):
    n_a, n_c, q_first = first_factor.shape
    n_b, n_d, q_second = second_factor.shape
    pairs = amplitudes.shape[0]
    size = n_c // CHUNKS
    far = ncol // 4
    whole = q_first * ndev
    some = pairs // ncol
    few = some // ndev
    width = n_a * n_b
    anywhere = pl.BlockSpec(memory_space=pl.ANY)
    dma = pltpu.SemaphoreType.DMA
    got = pl.pallas_call(
        functools.partial(kernel, ncol, ndev),
        out_shape=jax.ShapeDtypeStruct((few, width), jnp.float32),
        in_specs=[anywhere] * 3,
        out_specs=pl.BlockSpec(memory_space=pltpu.VMEM),
        scratch_shapes=[
            pltpu.VMEM((n_c, n_a, whole), jnp.bfloat16),
            pltpu.VMEM((n_b, n_d, whole), jnp.bfloat16),
            pltpu.VMEM((2, pairs, size, n_d), jnp.bfloat16),
            pltpu.VMEM((CHUNKS // 2, size, pairs, n_d), jnp.bfloat16),
            pltpu.VMEM((size, n_b, n_a, n_d), jnp.bfloat16),
            pltpu.VMEM((pairs, width), jnp.float32),
            pltpu.VMEM((ncol, some, width), jnp.float32),
            pltpu.VMEM((ndev, few, width), jnp.float32),
            pltpu.VMEM((ndev, few, width), jnp.float32),
            dma((2,)),
            dma((2, ndev - 1, CHUNKS)),
            dma((2, ndev - 1, CHUNKS)),
            dma((2, far, 2)),
            dma((2, far, 2)),
            dma((2, far + 1, 2)),
            dma((2, far + 1, 2)),
            dma((2,)),
            dma((ncol,)),
            dma((ncol,)),
            dma((ndev,)),
            dma((ndev,)),
        ],
        compiler_params=pltpu.CompilerParams(
            collective_id=0, has_side_effects=True, vmem_limit_bytes=58 * 2**20
        ),
    )(jnp.swapaxes(first_factor, 0, 1), second_factor, amplitudes)
    return jnp.swapaxes(got.reshape(few, n_b, n_a), 1, 2).reshape(few, width)


def solution(mesh):
    placed = (P(None, "col", "dev"), P(None, "dev", "col"), P(None, "col", "dev"))
    return jax.shard_map(
        functools.partial(on_device, mesh.shape["col"], mesh.shape["dev"]),
        mesh=mesh, in_specs=placed, out_specs=P(("col", "dev"), None), check_vma=False,
    )
```
